256 devices in a mesh: region: 8 (over x, core), sub: 32 (over z, y).
Axes of the slice: x: 4, y: 4, z: 8, core: 2. Of those that a mesh axis runs over, the one named last changes fastest.
Arguments:
- query_rows: bfloat16 [131072, 512], P(('region', 'sub')), parts along dimension 0, may hold values from -8 to 8
- key_rows: bfloat16 [131072, 512], P(('region', 'sub')), parts along dimension 0, may hold values from -8 to 8
- value_rows: bfloat16 [131072, 512], P(('region', 'sub')), parts along dimension 0, may hold values from -6 to 6
- grad_out: bfloat16 [131072, 512], P(('region', 'sub')), parts along dimension 0, may hold values from -6 to 6
- partner_balls: int32 [1024, 4], P('region'), parts along dimension 0, may hold values from 0 to 127, as said below
Outputs:
- grad_queries: bfloat16 [131072, 512], P(('region', 'sub')), parts along dimension 0
- grad_keys: bfloat16 [131072, 512], P(('region', 'sub')), parts along dimension 0
- grad_values: bfloat16 [131072, 512], P(('region', 'sub')), parts along dimension 0
The draws below stay inside these ranges and needn't reach their ends.
There are 8 independent parts, one for each index of `region`. The reference program is written for one: setup_inputs(seed, part) draws one part's arguments, and reference() takes and returns one part's arrays. A program takes and returns all parts, laid end to end along the dimension named above; each array names one. Nothing has to cross between parts.
Inputs may be any that keep to these rules, and one draw needn't show every extreme that they name: `partner_balls`: row b lists 4 distinct balls. Every listed ball lies in a subregion whose index differs from the index of b's subregion in exactly one bit; for every subregion s and each of the 5 subregions that differ from s in one bit, the balls of s together name exactly 1 distinct balls of that subregion.
All inputs are finite; a program needn't handle non-finite values.
Results may differ from the reference program's by a relative error of at most 0.0086.
Values may be sent and summed in bfloat16 or wider, within the bound.
A program may use at most 128 MiB of HBM per device.

```python
import math
import jax
import jax.numpy as jnp
from jax import lax

D = 512
HEADS = 8
HDIM = 64
BALL = 128
REMP = 4
SPHERES_IN_PATCH = 4
BITS = 5
CAP = 1
BALLS = 128
POINTS = 16384


def base_field(key, salt_value):
    row_count = BALLS * BALL
    scales = jnp.exp(jax.random.uniform(jax.random.fold_in(key, salt_value), (row_count, 1), minval=math.log(0.3), maxval=math.log(3.0)))
    field_values = jax.random.normal(jax.random.fold_in(key, salt_value + 1), (row_count, D)) * scales
    return jnp.clip(field_values, -8.0, 8.0)


def draw_query_rows(key, part):
    field_values = base_field(key, 10)
    return field_values.astype(jnp.bfloat16)


def draw_key_rows(key, part):
    field_values = base_field(key, 20)
    return field_values.astype(jnp.bfloat16)


def draw_partner_balls(key, part):
    sub_count = BALLS // SPHERES_IN_PATCH
    filled_total = BITS * CAP

    def one_sub(sub_index):
        sub_key = jax.random.fold_in(key, sub_index)
        bit_range = jnp.arange(BITS, dtype=jnp.int32)
        partner = jnp.bitwise_xor(sub_index, jnp.left_shift(jnp.int32(1), bit_range))

        def pick_balls(bit_index):
            return jax.random.permutation(jax.random.fold_in(sub_key, 100 + bit_index), SPHERES_IN_PATCH)[:CAP]
        chosen = jax.vmap(pick_balls)(bit_range)
        fetched = (partner[:, None] * SPHERES_IN_PATCH + chosen).reshape(-1)
        ball_order = jax.random.permutation(jax.random.fold_in(sub_key, 7), SPHERES_IN_PATCH)
        position_numbers = jnp.arange(filled_total, dtype=jnp.int32)
        mandatory_choice = ball_order[position_numbers % SPHERES_IN_PATCH]
        stochastic_jitter = jax.random.randint(jax.random.fold_in(sub_key, 9), (SPHERES_IN_PATCH, filled_total), 0, 65536)
        rating_increment = (mandatory_choice[None, :] == jnp.arange(SPHERES_IN_PATCH, dtype=jnp.int32)[:, None]).astype(jnp.int32) * (1 << 22)
        sphere_ratings = stochastic_jitter * filled_total + position_numbers[None, :] + rating_increment
        ignored, chosen_slots = lax.top_k(sphere_ratings, REMP)
        return fetched[chosen_slots]
    picked = jax.vmap(one_sub)(jnp.arange(sub_count, dtype=jnp.int32))
    return picked.reshape(BALLS, REMP).astype(jnp.int32)


def level_of(own_key, shape, pieces, smallest, largest):
    gain = 1.0
    for position, parts in pieces:
        steps = jax.random.uniform(jax.random.fold_in(jax.random.fold_in(own_key, 6), position), (parts,), jnp.float32, smallest / len(pieces), largest / len(pieces))
        gain = gain * jnp.repeat(jnp.exp(steps), shape[position] // parts).reshape((-1,) + (1,) * (len(shape) - 1 - position))
    return gain


def scatter_about(key, shape, deviation, bound, cuts=(), held_as=jnp.bfloat16):
    gain = level_of(key, shape, cuts, -0.22, 0.18) if cuts else 1.0
    result = jax.random.normal(key, shape, jnp.float32) * deviation * gain
    return jnp.minimum(jnp.maximum(result, -bound), bound).astype(held_as)


def setup_inputs(seed: int = 0, part: int = 0) -> dict:
    key_list = jax.random.split(jax.random.key(seed), 6)
    part_keys = jax.random.split(jax.random.fold_in(key_list[5], part), 6)
    query_rows = draw_query_rows(jax.random.fold_in(jax.random.fold_in(key_list[5], part), 71), part)
    key_rows = draw_key_rows(jax.random.fold_in(jax.random.fold_in(key_list[5], part), 71), part)
    value_rows = scatter_about(part_keys[2], (POINTS, D), 1.0, 6.0, ((0, 32),))
    grad_out = scatter_about(part_keys[3], (POINTS, D), 1.0, 6.0, ((0, 32),))
    partner_balls = draw_partner_balls(jax.random.fold_in(jax.random.fold_in(key_list[5], part), 71), part)
    return {"query_rows": query_rows, "key_rows": key_rows, "value_rows": value_rows, "grad_out": grad_out, "partner_balls": partner_balls}


def reference(query_rows, key_rows, value_rows, grad_out, partner_balls):
    sub_count = BALLS // SPHERES_IN_PATCH
    sub_rows = SPHERES_IN_PATCH * BALL
    score_scale = HDIM ** -0.5
    key_balls = key_rows.reshape(BALLS, BALL, HEADS, HDIM)
    value_balls = value_rows.reshape(BALLS, BALL, HEADS, HDIM)

    def per_sub(totals, sub_index):
        grad_k, grad_v = totals
        row_start = (sub_index * sub_rows).astype(jnp.int32)
        ball_start = (sub_index * SPHERES_IN_PATCH).astype(jnp.int32)
        near_query = lax.dynamic_slice_in_dim(query_rows, row_start, sub_rows, 0).reshape(SPHERES_IN_PATCH, BALL, HEADS, HDIM).astype(jnp.float32)
        near_grad = lax.dynamic_slice_in_dim(grad_out, row_start, sub_rows, 0).reshape(SPHERES_IN_PATCH, BALL, HEADS, HDIM).astype(jnp.float32)
        near_keys = lax.dynamic_slice_in_dim(key_rows, row_start, sub_rows, 0).reshape(sub_rows, HEADS, HDIM).astype(jnp.float32)
        near_values = lax.dynamic_slice_in_dim(value_rows, row_start, sub_rows, 0).reshape(sub_rows, HEADS, HDIM).astype(jnp.float32)
        partner = lax.dynamic_slice_in_dim(partner_balls, ball_start, SPHERES_IN_PATCH, 0).astype(jnp.int32)
        far_keys = key_balls[partner].reshape(SPHERES_IN_PATCH, REMP * BALL, HEADS, HDIM).astype(jnp.float32)
        far_values = value_balls[partner].reshape(SPHERES_IN_PATCH, REMP * BALL, HEADS, HDIM).astype(jnp.float32)
        near_scores = jnp.einsum('jqhd,khd->jhqk', near_query, near_keys) * score_scale
        far_scores = jnp.einsum('jqhd,jkhd->jhqk', near_query, far_keys) * score_scale
        row_max = jnp.maximum(jnp.max(near_scores, axis=-1), jnp.max(far_scores, axis=-1))
        row_sum = jnp.sum(jnp.exp(near_scores - row_max[..., None]), axis=-1) + jnp.sum(jnp.exp(far_scores - row_max[..., None]), axis=-1)
        log_norm = row_max + jnp.log(row_sum)
        near_probs = jnp.exp(near_scores - log_norm[..., None])
        far_probs = jnp.exp(far_scores - log_norm[..., None])
        near_pb = lax.optimization_barrier(near_probs.astype(jnp.bfloat16)).astype(jnp.float32)
        far_pb = lax.optimization_barrier(far_probs.astype(jnp.bfloat16)).astype(jnp.float32)
        attended = jnp.einsum('jhqk,khd->jqhd', near_pb, near_values) + jnp.einsum('jhqk,jkhd->jqhd', far_pb, far_values)
        delta = jnp.transpose(jnp.sum(near_grad * attended, axis=-1), (0, 2, 1))
        near_dp = jnp.einsum('jqhd,khd->jhqk', near_grad, near_values)
        far_dp = jnp.einsum('jqhd,jkhd->jhqk', near_grad, far_values)
        near_ds = lax.optimization_barrier((near_probs * (near_dp - delta[..., None])).astype(jnp.bfloat16)).astype(jnp.float32)
        far_ds = lax.optimization_barrier((far_probs * (far_dp - delta[..., None])).astype(jnp.bfloat16)).astype(jnp.float32)
        grad_q = (jnp.einsum('jhqk,khd->jqhd', near_ds, near_keys) + jnp.einsum('jhqk,jkhd->jqhd', far_ds, far_keys)) * score_scale
        grad_q = grad_q.reshape(sub_rows, D).astype(jnp.bfloat16)
        near_dk = jnp.einsum('jhqk,jqhd->khd', near_ds, near_query) * score_scale
        near_dv = jnp.einsum('jhqk,jqhd->khd', near_pb, near_grad)
        far_dk = (jnp.einsum('jhqk,jqhd->jkhd', far_ds, near_query) * score_scale).reshape(SPHERES_IN_PATCH * REMP, BALL, HEADS, HDIM)
        far_dv = jnp.einsum('jhqk,jqhd->jkhd', far_pb, near_grad).reshape(SPHERES_IN_PATCH * REMP, BALL, HEADS, HDIM)
        flat_partner = partner.reshape(-1)
        part_k = jnp.zeros((BALLS, BALL, HEADS, HDIM), jnp.float32).at[flat_partner].add(far_dk)
        part_v = jnp.zeros((BALLS, BALL, HEADS, HDIM), jnp.float32).at[flat_partner].add(far_dv)
        part_k = lax.optimization_barrier(part_k.astype(jnp.bfloat16)).astype(jnp.float32)
        part_v = lax.optimization_barrier(part_v.astype(jnp.bfloat16)).astype(jnp.float32)
        grad_k = grad_k + part_k.reshape(POINTS, D)
        grad_v = grad_v + part_v.reshape(POINTS, D)
        own_k = lax.dynamic_slice_in_dim(grad_k, row_start, sub_rows, 0) + near_dk.reshape(sub_rows, D)
        own_v = lax.dynamic_slice_in_dim(grad_v, row_start, sub_rows, 0) + near_dv.reshape(sub_rows, D)
        grad_k = lax.dynamic_update_slice_in_dim(grad_k, own_k, row_start, 0)
        grad_v = lax.dynamic_update_slice_in_dim(grad_v, own_v, row_start, 0)
        return (grad_k, grad_v), grad_q

    start_totals = (jnp.zeros((POINTS, D), jnp.float32), jnp.zeros((POINTS, D), jnp.float32))
    (grad_k, grad_v), grad_q = lax.scan(per_sub, start_totals, jnp.arange(sub_count, dtype=jnp.int32))
    return grad_q.reshape(POINTS, D), grad_k.astype(jnp.bfloat16), grad_v.astype(jnp.bfloat16)
```

```python
import functools

import jax
import jax.numpy as jnp
from jax import lax
from jax.experimental import pallas as pl
from jax.experimental.pallas import tpu as pltpu
from jax.sharding import PartitionSpec as P

HEADS = 8
HDIM = 64
BALL = 128
BALLS = 4
BITS = 5
ROWS = BALL * BALLS
WIDTH = HEADS * HDIM
SLAB = 2 * HDIM
PAIRS = HEADS // 2
FAR = BITS * BALL
KEYS = ROWS + FAR
QB = 256
UNITS = 2 * ROWS // QB
MESH = pl.DeviceIdType.MESH
SENDS = (4, 3, 2, 1, 0)
NN = (((1,), (0,)), ((), ()))
NT = (((1,), (1,)), ((), ()))


def mm(a, b, dims):
    return lax.dot_general(a, b, dims, preferred_element_type=jnp.float32)


def kernel(
    pb_ref, q_ref, k_ref, v_ref, g_ref, oq_ref, ok_ref, ov_ref,
    sbuf, rbuf, bsend, brecv, bias, rq, rg, kt, s_scr, dp_scr, p_scr, ds_scr,
    dqt, gk, gv, s_sem, r_sem, bs_sem, br_sem,
):
    region = lax.axis_index("region")
    me = lax.axis_index("sub")
    peers = [jnp.bitwise_xor(me, 1 << b) for b in range(BITS)]
    barrier = pltpu.get_barrier_semaphore()
    for peer in peers:
        pl.semaphore_signal(
            barrier, inc=1, device_id=(region, peer), device_id_type=MESH
        )

    named = []
    for b in range(BITS):
        ball = jnp.int32(0)
        for r in range(BALLS):
            for c in range(BALLS):
                entry = pb_ref[peers[b] * BALLS + r, c]
                ball = jnp.where(entry // BALLS == me, entry % BALLS, ball)
        named.append(ball)
    for b in SENDS:
        kb = k_ref[named[b]]
        vb = v_ref[named[b]]
        for p in range(PAIRS):
            sbuf[p, 0, b] = kb[:, p * SLAB : (p + 1) * SLAB]
            sbuf[p, 1, b] = vb[:, p * SLAB : (p + 1) * SLAB]

    def ahead(p, b):
        return pltpu.make_async_remote_copy(
            src_ref=sbuf.at[p, :, b],
            dst_ref=rbuf.at[p, :, b],
            send_sem=s_sem.at[p, b],
            recv_sem=r_sem.at[p, b],
            device_id=(region, peers[b]),
            device_id_type=MESH,
        )

    def back(p, b):
        return pltpu.make_async_remote_copy(
            src_ref=bsend.at[p, :, b],
            dst_ref=brecv.at[p, :, b],
            send_sem=bs_sem.at[p, b],
            recv_sem=br_sem.at[p, b],
            device_id=(region, peers[b]),
            device_id_type=MESH,
        )

    pl.semaphore_wait(barrier, BITS)

    @pl.loop(0, PAIRS)
    def _(p):
        for b in SENDS:
            ahead(p, b).start()

    for b in range(BITS):
        for r in range(BALLS):
            seen = jnp.float32(-1e30)
            for c in range(BALLS):
                entry = pb_ref[me * BALLS + r, c]
                seen = jnp.where(entry // BALLS == peers[b], jnp.float32(0), seen)
            bias[b, :, r * BALL : (r + 1) * BALL] = jnp.full((8, BALL), seen)

    lane = lax.broadcasted_iota(jnp.int32, (ROWS, SLAB), 1)

    @pl.loop(0, PAIRS)
    def _(p):
        cols = pl.ds(pl.multiple_of(p * SLAB, SLAB), SLAB)
        q = q_ref[:, cols] * jnp.bfloat16(HDIM**-0.5)
        g = g_ref[:, cols]
        zero = jnp.zeros_like(q)
        for hh in range(2):
            mine = (lane // HDIM) == hh
            rq[hh * ROWS : (hh + 1) * ROWS] = jnp.where(mine, q, zero)
            rg[hh * ROWS : (hh + 1) * ROWS] = jnp.where(mine, g, zero)
        for i in range(BALLS):
            kt[:, i * BALL : (i + 1) * BALL] = k_ref[i, :, cols].T
        for b in range(BITS):
            ahead(p, b).wait_recv()
        for b in range(BITS):
            kt[:, ROWS + b * BALL : ROWS + (b + 1) * BALL] = rbuf[p, 0, b].T

        def keys_of(i):
            return k_ref[i, :, cols] if i < BALLS else rbuf[p, 0, i - BALLS]

        def values_of(i):
            return v_ref[i, :, cols] if i < BALLS else rbuf[p, 1, i - BALLS]

        for u in range(UNITS):
            hh, qb = u // (ROWS // QB), u % (ROWS // QB)
            qu = rq[u * QB : (u + 1) * QB]
            gu = rg[u * QB : (u + 1) * QB]
            top = None
            for i in range(BALLS + BITS):
                s = mm(keys_of(i), qu, NT)
                if i >= BALLS:
                    s = s + bias[i - BALLS, 0:1, qb * QB : (qb + 1) * QB]
                s_scr[i] = s
                m = jnp.max(s.reshape(BALL // 8, 8, QB), axis=0)
                top = m if top is None else jnp.maximum(top, m)
            top = jnp.max(top, axis=0, keepdims=True)
            total = jnp.zeros((8, QB), jnp.float32)
            mean = jnp.zeros((8, QB), jnp.float32)
            for i in range(BALLS + BITS):
                dp = mm(values_of(i), gu, NT)
                e = jnp.exp(s_scr[i] - top)
                s_scr[i] = e
                dp_scr[i] = dp
                total = total + jnp.sum(e.reshape(BALL // 8, 8, QB), axis=0)
                mean = mean + jnp.sum((e * dp).reshape(BALL // 8, 8, QB), axis=0)
            scale = 1.0 / jnp.sum(total, axis=0, keepdims=True)
            delta = jnp.sum(mean, axis=0, keepdims=True) * scale
            at = slice(u * QB, (u + 1) * QB)
            for i in range(BALLS + BITS):
                pr = s_scr[i] * scale
                ds = pr * (dp_scr[i] - delta)
                p_scr[i * BALL : (i + 1) * BALL, at] = pr.astype(jnp.bfloat16)
                ds_scr[i * BALL : (i + 1) * BALL, at] = ds.astype(jnp.bfloat16)

        for b in range(BITS):
            at = slice(ROWS + b * BALL, ROWS + (b + 1) * BALL)
            bsend[p, 0, b] = mm(ds_scr[at], rq[...], NN).astype(jnp.bfloat16)
            bsend[p, 1, b] = mm(p_scr[at], rg[...], NN).astype(jnp.bfloat16)
        for b in SENDS:
            back(p, b).start()
        for i in range(BALLS):
            at = slice(i * BALL, (i + 1) * BALL)
            gk[p, i] = mm(ds_scr[at], rq[...], NN)
            gv[p, i] = mm(p_scr[at], rg[...], NN)
        for u in range(UNITS):
            hh, qb = u // (ROWS // QB), u % (ROWS // QB)
            dqt[hh * HDIM : (hh + 1) * HDIM, qb * QB : (qb + 1) * QB] = mm(
                kt[hh * HDIM : (hh + 1) * HDIM], ds_scr[:, u * QB : (u + 1) * QB], NN
            )
        oq_ref[:, cols] = (dqt[...].T * HDIM**-0.5).astype(jnp.bfloat16)

    share = [
        [jnp.where(named[b] == i, jnp.float32(1), jnp.float32(0)) for b in range(BITS)]
        for i in range(BALLS)
    ]

    @pl.loop(0, PAIRS)
    def _(p):
        cols = pl.ds(pl.multiple_of(p * SLAB, SLAB), SLAB)
        for b in range(BITS):
            back(p, b).wait_recv()
        for i in range(BALLS):
            ak, av = gk[p, i], gv[p, i]
            for b in range(BITS):
                ak = ak + share[i][b] * brecv[p, 0, b].astype(jnp.float32)
                av = av + share[i][b] * brecv[p, 1, b].astype(jnp.float32)
            ok_ref[i, :, cols] = ak.astype(jnp.bfloat16)
            ov_ref[i, :, cols] = av.astype(jnp.bfloat16)

    @pl.loop(0, PAIRS)
    def _(p):
        for b in range(BITS):
            ahead(p, b).wait_send()
            back(p, b).wait_send()


def body(query_rows, key_rows, value_rows, grad_out, partner_balls):
    vmem = pl.BlockSpec(memory_space=pltpu.VMEM)
    rows = jax.ShapeDtypeStruct((ROWS, WIDTH), jnp.bfloat16)
    balls = jax.ShapeDtypeStruct((BALLS, BALL, WIDTH), jnp.bfloat16)
    link = pltpu.VMEM((PAIRS, 2, BITS, BALL, SLAB), jnp.bfloat16)
    sem = pltpu.SemaphoreType.DMA((PAIRS, BITS))
    near = pltpu.VMEM((PAIRS, BALLS, BALL, SLAB), jnp.float32)
    grad_queries, grad_keys, grad_values = pl.pallas_call(
        kernel,
        out_shape=(rows, balls, balls),
        in_specs=[pl.BlockSpec(memory_space=pltpu.SMEM)] + [vmem] * 4,
        out_specs=(vmem, vmem, vmem),
        scratch_shapes=[
            link, link, link, link,
            pltpu.VMEM((BITS, 8, ROWS), jnp.float32),
            pltpu.VMEM((2 * ROWS, SLAB), jnp.bfloat16),
            pltpu.VMEM((2 * ROWS, SLAB), jnp.bfloat16),
            pltpu.VMEM((SLAB, KEYS), jnp.bfloat16),
            pltpu.VMEM((BALLS + BITS, BALL, QB), jnp.float32),
            pltpu.VMEM((BALLS + BITS, BALL, QB), jnp.float32),
            pltpu.VMEM((KEYS, 2 * ROWS), jnp.bfloat16),
            pltpu.VMEM((KEYS, 2 * ROWS), jnp.bfloat16),
            pltpu.VMEM((SLAB, ROWS), jnp.float32),
            near, near,
            sem, sem, sem, sem,
        ],
        compiler_params=pltpu.CompilerParams(
            collective_id=0, has_side_effects=True, vmem_limit_bytes=48 << 20
        ),
    )(
        partner_balls,
        query_rows,
        key_rows.reshape(BALLS, BALL, WIDTH),
        value_rows.reshape(BALLS, BALL, WIDTH),
        grad_out,
    )
    return (
        grad_queries,
        grad_keys.reshape(ROWS, WIDTH),
        grad_values.reshape(ROWS, WIDTH),
    )


def solution(mesh):
    rows = P(("region", "sub"), None)
    return jax.shard_map(
        body,
        mesh=mesh,
        in_specs=(rows, rows, rows, rows, P("region", None)),
        out_specs=(rows, rows, rows),
        check_vma=False,
    )
```

```python
import functools

import jax
import jax.numpy as jnp
from jax import lax
from jax.experimental import pallas as pl
from jax.experimental.pallas import tpu as pltpu
from jax.sharding import PartitionSpec as P

HEADS = 8
HDIM = 64
BALL = 128
BALLS = 4
BITS = 5
ROWS = BALL * BALLS
WIDTH = HEADS * HDIM
SLAB = 2 * HDIM
PAIRS = HEADS // 2
FAR = BITS * BALL
KEYS = ROWS + FAR
QB = 256
UNITS = 2 * ROWS // QB
MESH = pl.DeviceIdType.MESH
SENDS = (4, 3, 2, 1, 0)
NN = (((1,), (0,)), ((), ()))
NT = (((1,), (1,)), ((), ()))


def mm(a, b, dims):
    return lax.dot_general(a, b, dims, preferred_element_type=jnp.float32)


def kernel(
    pb_hbm, q_hbm, k_hbm, v_hbm, g_hbm, out,
    pb_ref, q_ref, k_ref, v_ref, g_ref, sbuf, rbuf, bsend, brecv, bias, rq, rg, kt, s_scr, dp_scr, p_scr, ds_scr,
    dqt, gk, gv, s_sem, r_sem, bs_sem, br_sem,
    pb_sem, in_sem,
):
    table = pltpu.make_async_copy(pb_hbm, pb_ref, pb_sem)
    table.start()
    fetch = [
        [
            pltpu.make_async_copy(src.at[i], dst.at[i], in_sem.at[n, i])
            for i in range(BALLS)
        ]
        for n, (src, dst) in enumerate(
            ((k_hbm, k_ref), (v_hbm, v_ref), (q_hbm, q_ref), (g_hbm, g_ref))
        )
    ]
    for copies in fetch:
        for copy in copies:
            copy.start()
    region = lax.axis_index("region")
    me = lax.axis_index("sub")
    peers = [jnp.bitwise_xor(me, 1 << b) for b in range(BITS)]
    barrier = pltpu.get_barrier_semaphore()
    for peer in peers:
        pl.semaphore_signal(
            barrier, inc=1, device_id=(region, peer), device_id_type=MESH
        )

    table.wait()
    named = []
    for b in range(BITS):
        ball = jnp.int32(0)
        for r in range(BALLS):
            for c in range(BALLS):
                entry = pb_ref[c, peers[b] * BALLS + r]
                ball = jnp.where(entry // BALLS == me, entry % BALLS, ball)
        named.append(ball)
    for copies in fetch[:2]:
        for copy in copies:
            copy.wait()
    for b in SENDS:
        kb = k_ref[named[b]]
        vb = v_ref[named[b]]
        for p in range(PAIRS):
            sbuf[p, 0, b] = kb[:, p * SLAB : (p + 1) * SLAB]
            sbuf[p, 1, b] = vb[:, p * SLAB : (p + 1) * SLAB]

    def ahead(p, b):
        return pltpu.make_async_remote_copy(
            src_ref=sbuf.at[p, :, b],
            dst_ref=rbuf.at[p, :, b],
            send_sem=s_sem.at[p, b],
            recv_sem=r_sem.at[p, b],
            device_id=(region, peers[b]),
            device_id_type=MESH,
        )

    def back(p, b):
        return pltpu.make_async_remote_copy(
            src_ref=bsend.at[p, :, b],
            dst_ref=brecv.at[p, :, b],
            send_sem=bs_sem.at[p, b],
            recv_sem=br_sem.at[p, b],
            device_id=(region, peers[b]),
            device_id_type=MESH,
        )

    pl.semaphore_wait(barrier, BITS)

    @pl.loop(0, PAIRS)
    def _(p):
        for b in SENDS:
            ahead(p, b).start()

    for b in range(BITS):
        for r in range(BALLS):
            seen = jnp.float32(-1e30)
            for c in range(BALLS):
                entry = pb_ref[c, me * BALLS + r]
                seen = jnp.where(entry // BALLS == peers[b], jnp.float32(0), seen)
            bias[b, :, r * BALL : (r + 1) * BALL] = jnp.full((8, BALL), seen)

    for copies in fetch[2:]:
        for copy in copies:
            copy.wait()
    lane = lax.broadcasted_iota(jnp.int32, (ROWS, SLAB), 1)

    @pl.loop(0, PAIRS)
    def _(p):
        cols = pl.ds(pl.multiple_of(p * SLAB, SLAB), SLAB)
        q = q_ref[:, :, cols].reshape(ROWS, SLAB) * jnp.bfloat16(HDIM**-0.5)
        g = g_ref[:, :, cols].reshape(ROWS, SLAB)
        zero = jnp.zeros_like(q)
        for hh in range(2):
            mine = (lane // HDIM) == hh
            rq[hh * ROWS : (hh + 1) * ROWS] = jnp.where(mine, q, zero)
            rg[hh * ROWS : (hh + 1) * ROWS] = jnp.where(mine, g, zero)
        for i in range(BALLS):
            kt[:, i * BALL : (i + 1) * BALL] = k_ref[i, :, cols].T
        for b in range(BITS):
            ahead(p, b).wait_recv()
        for b in range(BITS):
            kt[:, ROWS + b * BALL : ROWS + (b + 1) * BALL] = rbuf[p, 0, b].T

        def keys_of(i):
            return k_ref[i, :, cols] if i < BALLS else rbuf[p, 0, i - BALLS]

        def values_of(i):
            return v_ref[i, :, cols] if i < BALLS else rbuf[p, 1, i - BALLS]

        for u in range(UNITS):
            hh, qb = u // (ROWS // QB), u % (ROWS // QB)
            qu = rq[u * QB : (u + 1) * QB]
            gu = rg[u * QB : (u + 1) * QB]
            top = None
            for i in range(BALLS + BITS):
                s = mm(keys_of(i), qu, NT)
                if i >= BALLS:
                    s = s + bias[i - BALLS, 0:1, qb * QB : (qb + 1) * QB]
                s_scr[i] = s
                m = jnp.max(s.reshape(BALL // 8, 8, QB), axis=0)
                top = m if top is None else jnp.maximum(top, m)
            top = jnp.max(top, axis=0, keepdims=True)
            total = jnp.zeros((8, QB), jnp.float32)
            mean = jnp.zeros((8, QB), jnp.float32)
            for i in range(BALLS + BITS):
                dp = mm(values_of(i), gu, NT)
                e = jnp.exp(s_scr[i] - top)
                s_scr[i] = e
                dp_scr[i] = dp
                total = total + jnp.sum(e.reshape(BALL // 8, 8, QB), axis=0)
                mean = mean + jnp.sum((e * dp).reshape(BALL // 8, 8, QB), axis=0)
            scale = 1.0 / jnp.sum(total, axis=0, keepdims=True)
            delta = jnp.sum(mean, axis=0, keepdims=True) * scale
            at = slice(u * QB, (u + 1) * QB)
            for i in range(BALLS + BITS):
                pr = s_scr[i] * scale
                ds = pr * (dp_scr[i] - delta)
                p_scr[i * BALL : (i + 1) * BALL, at] = pr.astype(jnp.bfloat16)
                ds_scr[i * BALL : (i + 1) * BALL, at] = ds.astype(jnp.bfloat16)

        for b in range(BITS):
            at = slice(ROWS + b * BALL, ROWS + (b + 1) * BALL)
            bsend[p, 0, b] = mm(ds_scr[at], rq[...], NN).astype(jnp.bfloat16)
            bsend[p, 1, b] = mm(p_scr[at], rg[...], NN).astype(jnp.bfloat16)
        for b in SENDS:
            back(p, b).start()
        for i in range(BALLS):
            at = slice(i * BALL, (i + 1) * BALL)
            gk[p, i] = mm(ds_scr[at], rq[...], NN)
            gv[p, i] = mm(p_scr[at], rg[...], NN)
        for u in range(UNITS):
            hh, qb = u // (ROWS // QB), u % (ROWS // QB)
            dqt[hh * HDIM : (hh + 1) * HDIM, qb * QB : (qb + 1) * QB] = mm(
                kt[hh * HDIM : (hh + 1) * HDIM], ds_scr[:, u * QB : (u + 1) * QB], NN
            )
        for i in range(BALLS):
            dq = dqt[:, i * BALL : (i + 1) * BALL].T * HDIM**-0.5
            out[0, i, :, cols] = dq.astype(jnp.bfloat16)

    share = [
        [jnp.where(named[b] == i, jnp.float32(1), jnp.float32(0)) for b in range(BITS)]
        for i in range(BALLS)
    ]

    @pl.loop(0, PAIRS)
    def _(p):
        cols = pl.ds(pl.multiple_of(p * SLAB, SLAB), SLAB)
        for b in range(BITS):
            back(p, b).wait_recv()
        for i in range(BALLS):
            ak, av = gk[p, i], gv[p, i]
            for b in range(BITS):
                ak = ak + share[i][b] * brecv[p, 0, b].astype(jnp.float32)
                av = av + share[i][b] * brecv[p, 1, b].astype(jnp.float32)
            out[1, i, :, cols] = ak.astype(jnp.bfloat16)
            out[2, i, :, cols] = av.astype(jnp.bfloat16)

    @pl.loop(0, PAIRS)
    def _(p):
        for b in range(BITS):
            ahead(p, b).wait_send()
            back(p, b).wait_send()


def deliver(grads, oq_ref, ok_ref, ov_ref, sem):
    copies = [
        pltpu.make_async_copy(grads.at[n, i], dst.at[i], sem.at[n, i])
        for n, dst in enumerate((oq_ref, ok_ref, ov_ref))
        for i in range(BALLS)
    ]
    for copy in copies:
        copy.start()
    for copy in copies:
        copy.wait()


def body(query_rows, key_rows, value_rows, grad_out, partner_balls):
    vmem = pl.BlockSpec(memory_space=pltpu.VMEM)
    hbm = pl.BlockSpec(memory_space=pltpu.HBM)
    balls = jax.ShapeDtypeStruct((BALLS, BALL, WIDTH), jnp.bfloat16)
    link = pltpu.VMEM((PAIRS, 2, BITS, BALL, SLAB), jnp.bfloat16)
    sem = pltpu.SemaphoreType.DMA((PAIRS, BITS))
    near = pltpu.VMEM((PAIRS, BALLS, BALL, SLAB), jnp.float32)
    rows = pltpu.VMEM((BALLS, BALL, WIDTH), jnp.bfloat16)
    grads = pl.pallas_call(
        kernel,
        out_shape=pltpu.VMEM((3, BALLS, BALL, WIDTH), jnp.bfloat16),
        in_specs=[hbm] * 5,
        out_specs=vmem,
        scratch_shapes=[
            pltpu.SMEM((BALLS, BALLS * 32), jnp.int32),
            rows, rows, rows, rows,
            link, link, link, link,
            pltpu.VMEM((BITS, 8, ROWS), jnp.float32),
            pltpu.VMEM((2 * ROWS, SLAB), jnp.bfloat16),
            pltpu.VMEM((2 * ROWS, SLAB), jnp.bfloat16),
            pltpu.VMEM((SLAB, KEYS), jnp.bfloat16),
            pltpu.VMEM((BALLS + BITS, BALL, QB), jnp.float32),
            pltpu.VMEM((BALLS + BITS, BALL, QB), jnp.float32),
            pltpu.VMEM((KEYS, 2 * ROWS), jnp.bfloat16),
            pltpu.VMEM((KEYS, 2 * ROWS), jnp.bfloat16),
            pltpu.VMEM((SLAB, ROWS), jnp.float32),
            near, near,
            sem, sem, sem, sem,
            pltpu.SemaphoreType.DMA,
            pltpu.SemaphoreType.DMA((4, BALLS)),
        ],
        compiler_params=pltpu.CompilerParams(
            collective_id=0, has_side_effects=True, vmem_limit_bytes=40 << 20
        ),
    )(
        pltpu.with_memory_space_constraint(partner_balls.T, pltpu.HBM),
        *(
            pltpu.with_memory_space_constraint(
                x.reshape(BALLS, BALL, WIDTH), pltpu.HBM
            )
            for x in (query_rows, key_rows, value_rows, grad_out)
        ),
    )
    grads = pl.pallas_call(
        deliver,
        out_shape=(balls, balls, balls),
        in_specs=[vmem],
        out_specs=(hbm, hbm, hbm),
        scratch_shapes=[pltpu.SemaphoreType.DMA((3, BALLS))],
        compiler_params=pltpu.CompilerParams(vmem_limit_bytes=8 << 20),
    )(pltpu.with_memory_space_constraint(grads, pltpu.VMEM))
    return tuple(x.reshape(ROWS, WIDTH) for x in grads)


def solution(mesh):
    rows = P(("region", "sub"), None)
    return jax.shard_map(
        body,
        mesh=mesh,
        in_specs=(rows, rows, rows, rows, P("region", None)),
        out_specs=(rows, rows, rows),
        check_vma=False,
    )
```

```python
import functools

import jax
import jax.numpy as jnp
from jax import lax
from jax.experimental import pallas as pl
from jax.experimental.pallas import tpu as pltpu
from jax.sharding import PartitionSpec as P

HEADS = 8
HDIM = 64
BALL = 128
BALLS = 4
BITS = 5
ROWS = BALL * BALLS
WIDTH = HEADS * HDIM
SLAB = 2 * HDIM
PAIRS = HEADS // 2
FAR = BITS * BALL
KEYS = ROWS + FAR
QB = 256
UNITS = 2 * ROWS // QB
MESH = pl.DeviceIdType.MESH
SENDS = (4, 3, 2, 1, 0)
NN = (((1,), (0,)), ((), ()))
NT = (((1,), (1,)), ((), ()))


def mm(a, b, dims):
    return lax.dot_general(a, b, dims, preferred_element_type=jnp.float32)


def kernel(
    pb_hbm, q_hbm, k_hbm, v_hbm, g_hbm, out,
    pb_ref, q_ref, k_ref, v_ref, g_ref, sbuf, rbuf, bsend, brecv, bias, rq, rg, kt, s_scr, dp_scr, p_scr, ds_scr,
    dqt, gk, gv, s_sem, r_sem, bs_sem, br_sem,
    pb_sem, in_sem,
):
    table = pltpu.make_async_copy(pb_hbm, pb_ref, pb_sem)
    table.start()
    fetch = [
        [
            pltpu.make_async_copy(src.at[i], dst.at[i], in_sem.at[n, i])
            for i in range(BALLS)
        ]
        for n, (src, dst) in enumerate(
            ((k_hbm, k_ref), (v_hbm, v_ref), (q_hbm, q_ref), (g_hbm, g_ref))
        )
    ]
    for copies in fetch[:2]:
        for copy in copies:
            copy.start()
    region = lax.axis_index("region")
    me = lax.axis_index("sub")
    peers = [jnp.bitwise_xor(me, 1 << b) for b in range(BITS)]
    barrier = pltpu.get_barrier_semaphore()
    for peer in peers:
        pl.semaphore_signal(
            barrier, inc=1, device_id=(region, peer), device_id_type=MESH
        )

    table.wait()
    named = []
    for b in range(BITS):
        ball = jnp.int32(0)
        for r in range(BALLS):
            for c in range(BALLS):
                entry = pb_ref[c, peers[b] * BALLS + r]
                ball = jnp.where(entry // BALLS == me, entry % BALLS, ball)
        named.append(ball)
    for copies in fetch[:2]:
        for copy in copies:
            copy.wait()
    for copies in fetch[2:]:
        for copy in copies:
            copy.start()
    for b in SENDS:
        kb = k_ref[named[b]]
        vb = v_ref[named[b]]
        for p in range(PAIRS):
            sbuf[p, 0, b] = kb[:, p * SLAB : (p + 1) * SLAB]
            sbuf[p, 1, b] = vb[:, p * SLAB : (p + 1) * SLAB]

    def ahead(p, b):
        return pltpu.make_async_remote_copy(
            src_ref=sbuf.at[p, :, b],
            dst_ref=rbuf.at[p, :, b],
            send_sem=s_sem.at[p, b],
            recv_sem=r_sem.at[p, b],
            device_id=(region, peers[b]),
            device_id_type=MESH,
        )

    def back(p, b):
        return pltpu.make_async_remote_copy(
            src_ref=bsend.at[p, :, b],
            dst_ref=brecv.at[p, :, b],
            send_sem=bs_sem.at[p, b],
            recv_sem=br_sem.at[p, b],
            device_id=(region, peers[b]),
            device_id_type=MESH,
        )

    pl.semaphore_wait(barrier, BITS)

    @pl.loop(0, PAIRS)
    def _(p):
        for b in SENDS:
            ahead(p, b).start()

    for b in range(BITS):
        for r in range(BALLS):
            seen = jnp.float32(-1e30)
            for c in range(BALLS):
                entry = pb_ref[c, me * BALLS + r]
                seen = jnp.where(entry // BALLS == peers[b], jnp.float32(0), seen)
            bias[b, :, r * BALL : (r + 1) * BALL] = jnp.full((8, BALL), seen)

    for copies in fetch[2:]:
        for copy in copies:
            copy.wait()
    lane = lax.broadcasted_iota(jnp.int32, (ROWS, SLAB), 1)

    @pl.loop(0, PAIRS)
    def _(p):
        cols = pl.ds(pl.multiple_of(p * SLAB, SLAB), SLAB)
        q = q_ref[:, :, cols].reshape(ROWS, SLAB) * jnp.bfloat16(HDIM**-0.5)
        g = g_ref[:, :, cols].reshape(ROWS, SLAB)
        zero = jnp.zeros_like(q)
        for hh in range(2):
            mine = (lane // HDIM) == hh
            rq[hh * ROWS : (hh + 1) * ROWS] = jnp.where(mine, q, zero)
            rg[hh * ROWS : (hh + 1) * ROWS] = jnp.where(mine, g, zero)
        for i in range(BALLS):
            kt[:, i * BALL : (i + 1) * BALL] = k_ref[i, :, cols].T
        for b in range(BITS):
            ahead(p, b).wait_recv()
        for b in range(BITS):
            kt[:, ROWS + b * BALL : ROWS + (b + 1) * BALL] = rbuf[p, 0, b].T

        def keys_of(i):
            return k_ref[i, :, cols] if i < BALLS else rbuf[p, 0, i - BALLS]

        def values_of(i):
            return v_ref[i, :, cols] if i < BALLS else rbuf[p, 1, i - BALLS]

        @pl.loop(0, UNITS)
        def _(u):
            hh, qb = u // (ROWS // QB), u % (ROWS // QB)
            at = pl.ds(pl.multiple_of(u * QB, QB), QB)
            some = pl.ds(pl.multiple_of(qb * QB, QB), QB)
            head = pl.ds(pl.multiple_of(hh * HDIM, HDIM), HDIM)
            qu = rq[at]
            gu = rg[at]
            top = None
            for i in range(BALLS + BITS):
                s = mm(keys_of(i), qu, NT)
                if i >= BALLS:
                    s = s + bias[i - BALLS, 0:1, some]
                s_scr[i] = s
                m = jnp.max(s.reshape(BALL // 8, 8, QB), axis=0)
                top = m if top is None else jnp.maximum(top, m)
            top = jnp.max(top, axis=0, keepdims=True)
            total = jnp.zeros((8, QB), jnp.float32)
            for i in range(BALLS + BITS):
                dp = mm(values_of(i), gu, NT)
                e = jnp.exp(s_scr[i] - top)
                s_scr[i] = e
                dp_scr[i] = dp
                total = total + jnp.sum(e.reshape(BALL // 8, 8, QB), axis=0)
            scale = 1.0 / jnp.sum(total, axis=0, keepdims=True)
            mean = jnp.zeros((8, QB), jnp.float32)
            for i in range(BALLS + BITS):
                pb = (s_scr[i] * scale).astype(jnp.bfloat16)
                p_scr[i * BALL : (i + 1) * BALL, at] = pb
                part = pb.astype(jnp.float32) * dp_scr[i]
                mean = mean + jnp.sum(part.reshape(BALL // 8, 8, QB), axis=0)
            delta = jnp.sum(mean, axis=0, keepdims=True)
            for i in range(BALLS + BITS):
                ds = s_scr[i] * scale * (dp_scr[i] - delta)
                ds_scr[i * BALL : (i + 1) * BALL, at] = ds.astype(jnp.bfloat16)
            dqt[head, some] = mm(kt[head], ds_scr[:, at], NN)

        for b in range(BITS):
            at = slice(ROWS + b * BALL, ROWS + (b + 1) * BALL)
            bsend[p, 0, b] = mm(ds_scr[at], rq[...], NN).astype(jnp.bfloat16)
            bsend[p, 1, b] = mm(p_scr[at], rg[...], NN).astype(jnp.bfloat16)
        for b in SENDS:
            back(p, b).start()
        for i in range(BALLS):
            at = slice(i * BALL, (i + 1) * BALL)
            gk[p, i] = mm(ds_scr[at], rq[...], NN)
            gv[p, i] = mm(p_scr[at], rg[...], NN)
        for i in range(BALLS):
            dq = dqt[:, i * BALL : (i + 1) * BALL].T * HDIM**-0.5
            out[0, i, :, cols] = dq.astype(jnp.bfloat16)

    share = [
        [jnp.where(named[b] == i, jnp.float32(1), jnp.float32(0)) for b in range(BITS)]
        for i in range(BALLS)
    ]

    @pl.loop(0, PAIRS)
    def _(p):
        cols = pl.ds(pl.multiple_of(p * SLAB, SLAB), SLAB)
        for b in range(BITS):
            back(p, b).wait_recv()
        for i in range(BALLS):
            ak, av = gk[p, i], gv[p, i]
            for b in range(BITS):
                ak = ak + share[i][b] * brecv[p, 0, b].astype(jnp.float32)
                av = av + share[i][b] * brecv[p, 1, b].astype(jnp.float32)
            out[1, i, :, cols] = ak.astype(jnp.bfloat16)
            out[2, i, :, cols] = av.astype(jnp.bfloat16)

    @pl.loop(0, PAIRS)
    def _(p):
        for b in range(BITS):
            ahead(p, b).wait_send()
            back(p, b).wait_send()


def deliver(grads, oq_ref, ok_ref, ov_ref, sem):
    copies = [
        pltpu.make_async_copy(grads.at[n, i], dst.at[i], sem.at[n, i])
        for n, dst in enumerate((oq_ref, ok_ref, ov_ref))
        for i in range(BALLS)
    ]
    for copy in copies:
        copy.start()
    for copy in copies:
        copy.wait()


def body(query_rows, key_rows, value_rows, grad_out, partner_balls):
    vmem = pl.BlockSpec(memory_space=pltpu.VMEM)
    hbm = pl.BlockSpec(memory_space=pltpu.HBM)
    balls = jax.ShapeDtypeStruct((BALLS, BALL, WIDTH), jnp.bfloat16)
    link = pltpu.VMEM((PAIRS, 2, BITS, BALL, SLAB), jnp.bfloat16)
    sem = pltpu.SemaphoreType.DMA((PAIRS, BITS))
    near = pltpu.VMEM((PAIRS, BALLS, BALL, SLAB), jnp.float32)
    rows = pltpu.VMEM((BALLS, BALL, WIDTH), jnp.bfloat16)
    grads = pl.pallas_call(
        kernel,
        out_shape=pltpu.VMEM((3, BALLS, BALL, WIDTH), jnp.bfloat16),
        in_specs=[hbm] * 5,
        out_specs=vmem,
        scratch_shapes=[
            pltpu.SMEM((BALLS, BALLS * 32), jnp.int32),
            rows, rows, rows, rows,
            link, link, link, link,
            pltpu.VMEM((BITS, 8, ROWS), jnp.float32),
            pltpu.VMEM((2 * ROWS, SLAB), jnp.bfloat16),
            pltpu.VMEM((2 * ROWS, SLAB), jnp.bfloat16),
            pltpu.VMEM((SLAB, KEYS), jnp.bfloat16),
            pltpu.VMEM((BALLS + BITS, BALL, QB), jnp.float32),
            pltpu.VMEM((BALLS + BITS, BALL, QB), jnp.float32),
            pltpu.VMEM((KEYS, 2 * ROWS), jnp.bfloat16),
            pltpu.VMEM((KEYS, 2 * ROWS), jnp.bfloat16),
            pltpu.VMEM((SLAB, ROWS), jnp.float32),
            near, near,
            sem, sem, sem, sem,
            pltpu.SemaphoreType.DMA,
            pltpu.SemaphoreType.DMA((4, BALLS)),
        ],
        compiler_params=pltpu.CompilerParams(
            collective_id=0, has_side_effects=True, vmem_limit_bytes=40 << 20
        ),
    )(
        pltpu.with_memory_space_constraint(partner_balls.T, pltpu.HBM),
        *(
            pltpu.with_memory_space_constraint(
                x.reshape(BALLS, BALL, WIDTH), pltpu.HBM
            )
            for x in (query_rows, key_rows, value_rows, grad_out)
        ),
    )
    grads = pl.pallas_call(
        deliver,
        out_shape=(balls, balls, balls),
        in_specs=[vmem],
        out_specs=(hbm, hbm, hbm),
        scratch_shapes=[pltpu.SemaphoreType.DMA((3, BALLS))],
        compiler_params=pltpu.CompilerParams(vmem_limit_bytes=8 << 20),
    )(pltpu.with_memory_space_constraint(grads, pltpu.VMEM))
    return tuple(x.reshape(ROWS, WIDTH) for x in grads)


def solution(mesh):
    rows = P(("region", "sub"), None)
    return jax.shard_map(
        body,
        mesh=mesh,
        in_specs=(rows, rows, rows, rows, P("region", None)),
        out_specs=(rows, rows, rows),
        check_vma=False,
    )
```

```python
import functools

import jax
import jax.numpy as jnp
from jax import lax
from jax.experimental import pallas as pl
from jax.experimental.pallas import tpu as pltpu
from jax.sharding import PartitionSpec as P

HEADS = 8
HDIM = 64
BALL = 128
BALLS = 4
BITS = 5
ROWS = BALL * BALLS
WIDTH = HEADS * HDIM
SLAB = 2 * HDIM
PAIRS = HEADS // 2
FAR = BITS * BALL
KEYS = ROWS + FAR
QB = 256
UNITS = 2 * ROWS // QB
MESH = pl.DeviceIdType.MESH
SENDS = (4, 3, 2, 1, 0)
NN = (((1,), (0,)), ((), ()))
NT = (((1,), (1,)), ((), ()))


def mm(a, b, dims):
    return lax.dot_general(a, b, dims, preferred_element_type=jnp.float32)


def kernel(
    pb_hbm, q_hbm, k_hbm, v_hbm, g_hbm, out,
    pb_ref, q_ref, k_ref, v_ref, g_ref, sbuf, rbuf, bsend, brecv, bias, rq, rg, kt, s_scr, dp_scr, p_scr, ds_scr,
    dqt, gk, gv, s_sem, r_sem, bs_sem, br_sem,
    pb_sem, in_sem,
):
    table = pltpu.make_async_copy(pb_hbm, pb_ref, pb_sem)
    table.start()
    fetch = [
        [
            pltpu.make_async_copy(src.at[i], dst.at[i], in_sem.at[n, i])
            for i in range(BALLS)
        ]
        for n, (src, dst) in enumerate(
            ((k_hbm, k_ref), (v_hbm, v_ref), (q_hbm, q_ref), (g_hbm, g_ref))
        )
    ]
    for copies in fetch[:2]:
        for copy in copies:
            copy.start()
    region = lax.axis_index("region")
    me = lax.axis_index("sub")
    deep = me // 4
    peers = [jnp.bitwise_xor(me, 1 << b) for b in range(BITS)]
    barrier = pltpu.get_barrier_semaphore()
    for peer in peers:
        pl.semaphore_signal(
            barrier, inc=1, device_id=(region, peer), device_id_type=MESH
        )

    table.wait()
    named = []
    for b in range(BITS):
        ball = jnp.int32(0)
        for r in range(BALLS):
            for c in range(BALLS):
                entry = pb_ref[c, peers[b] * BALLS + r]
                ball = jnp.where(entry // BALLS == me, entry % BALLS, ball)
        named.append(ball)
    for copies in fetch[:2]:
        for copy in copies:
            copy.wait()
    for copies in fetch[2:]:
        for copy in copies:
            copy.start()
    for b in SENDS:
        kb = k_ref[named[b]]
        vb = v_ref[named[b]]
        for p in range(PAIRS):
            sbuf[p, 0, b] = kb[:, p * SLAB : (p + 1) * SLAB]
            sbuf[p, 1, b] = vb[:, p * SLAB : (p + 1) * SLAB]

    def ahead(p, b):
        return pltpu.make_async_remote_copy(
            src_ref=sbuf.at[p, :, b],
            dst_ref=rbuf.at[p, :, b],
            send_sem=s_sem.at[p, b],
            recv_sem=r_sem.at[p, b],
            device_id=(region, peers[b]),
            device_id_type=MESH,
        )

    def back(p, b):
        return pltpu.make_async_remote_copy(
            src_ref=bsend.at[p, :, b],
            dst_ref=brecv.at[p, :, b],
            send_sem=bs_sem.at[p, b],
            recv_sem=br_sem.at[p, b],
            device_id=(region, peers[b]),
            device_id_type=MESH,
        )

    def give_near(p):
        for b in (3, 2):

            @pl.when(deep // (1 << (b - 2)) % 2 == 1)
            def _():
                back(p, b).start()

        for b in (1, 0):
            back(p, b).start()
        for b in (2, 3):

            @pl.when(deep // (1 << (b - 2)) % 2 == 0)
            def _():
                back(p, b).start()

    def give_late(p):
        @pl.when(deep < 4)
        def _():
            back(p, 4).start()

        @pl.when(deep >= 4)
        def _():
            give_near(p)

    def serve(p, copy, bits):
        for b in (4, 3, 2):

            @pl.when(deep // (1 << (b - 2)) % 2 == 1)
            def _():
                copy(p, b).start()

        for b in bits:
            copy(p, b).start()
        for b in (2, 3, 4):

            @pl.when(deep // (1 << (b - 2)) % 2 == 0)
            def _():
                copy(p, b).start()

    pl.semaphore_wait(barrier, BITS)

    @pl.loop(0, PAIRS)
    def _(p):
        serve(p, ahead, (1, 0))

    for b in range(BITS):
        for r in range(BALLS):
            seen = jnp.float32(-1e30)
            for c in range(BALLS):
                entry = pb_ref[c, me * BALLS + r]
                seen = jnp.where(entry // BALLS == peers[b], jnp.float32(0), seen)
            bias[b, :, r * BALL : (r + 1) * BALL] = jnp.full((8, BALL), seen)

    for copies in fetch[2:]:
        for copy in copies:
            copy.wait()
    lane = lax.broadcasted_iota(jnp.int32, (ROWS, SLAB), 1)

    @pl.loop(0, PAIRS)
    def _(p):
        cols = pl.ds(pl.multiple_of(p * SLAB, SLAB), SLAB)
        q = q_ref[:, :, cols].reshape(ROWS, SLAB) * jnp.bfloat16(HDIM**-0.5)
        g = g_ref[:, :, cols].reshape(ROWS, SLAB)
        zero = jnp.zeros_like(q)
        for hh in range(2):
            mine = (lane // HDIM) == hh
            rq[hh * ROWS : (hh + 1) * ROWS] = jnp.where(mine, q, zero)
            rg[hh * ROWS : (hh + 1) * ROWS] = jnp.where(mine, g, zero)
        for i in range(BALLS):
            kt[:, i * BALL : (i + 1) * BALL] = k_ref[i, :, cols].T
        for b in range(BITS):
            ahead(p, b).wait_recv()
        for b in range(BITS):
            kt[:, ROWS + b * BALL : ROWS + (b + 1) * BALL] = rbuf[p, 0, b].T

        def keys_of(i):
            return k_ref[i, :, cols] if i < BALLS else rbuf[p, 0, i - BALLS]

        def values_of(i):
            return v_ref[i, :, cols] if i < BALLS else rbuf[p, 1, i - BALLS]

        @pl.loop(0, UNITS)
        def _(u):
            hh, qb = u // (ROWS // QB), u % (ROWS // QB)
            at = pl.ds(pl.multiple_of(u * QB, QB), QB)
            some = pl.ds(pl.multiple_of(qb * QB, QB), QB)
            head = pl.ds(pl.multiple_of(hh * HDIM, HDIM), HDIM)
            qu = rq[at]
            gu = rg[at]
            top = None
            for i in range(BALLS + BITS):
                s = mm(keys_of(i), qu, NT)
                if i >= BALLS:
                    s = s + bias[i - BALLS, 0:1, some]
                s_scr[i] = s
                m = jnp.max(s.reshape(BALL // 8, 8, QB), axis=0)
                top = m if top is None else jnp.maximum(top, m)
            top = jnp.max(top, axis=0, keepdims=True)
            total = jnp.zeros((8, QB), jnp.float32)
            for i in range(BALLS + BITS):
                dp = mm(values_of(i), gu, NT)
                e = jnp.exp(s_scr[i] - top)
                s_scr[i] = e
                dp_scr[i] = dp
                total = total + jnp.sum(e.reshape(BALL // 8, 8, QB), axis=0)
            scale = 1.0 / jnp.sum(total, axis=0, keepdims=True)
            mean = jnp.zeros((8, QB), jnp.float32)
            for i in range(BALLS + BITS):
                pb = (s_scr[i] * scale).astype(jnp.bfloat16)
                p_scr[i * BALL : (i + 1) * BALL, at] = pb
                part = pb.astype(jnp.float32) * dp_scr[i]
                mean = mean + jnp.sum(part.reshape(BALL // 8, 8, QB), axis=0)
            delta = jnp.sum(mean, axis=0, keepdims=True)
            for i in range(BALLS + BITS):
                ds = s_scr[i] * scale * (dp_scr[i] - delta)
                ds_scr[i * BALL : (i + 1) * BALL, at] = ds.astype(jnp.bfloat16)
            dqt[head, some] = mm(kt[head], ds_scr[:, at], NN)

        for b in range(BITS):
            at = slice(ROWS + b * BALL, ROWS + (b + 1) * BALL)
            bsend[p, 0, b] = mm(ds_scr[at], rq[...], NN).astype(jnp.bfloat16)
            bsend[p, 1, b] = mm(p_scr[at], rg[...], NN).astype(jnp.bfloat16)
        @pl.when(deep < 4)
        def _():
            give_near(p)

        @pl.when(deep >= 4)
        def _():
            back(p, 4).start()

        @pl.when(p > 0)
        def _():
            give_late(p - 1)

        @pl.when(p == PAIRS - 1)
        def _():
            give_late(p)

        for i in range(BALLS):
            at = slice(i * BALL, (i + 1) * BALL)
            gk[p, i] = mm(ds_scr[at], rq[...], NN)
            gv[p, i] = mm(p_scr[at], rg[...], NN)
        for i in range(BALLS):
            dq = dqt[:, i * BALL : (i + 1) * BALL].T * HDIM**-0.5
            out[0, i, :, cols] = dq.astype(jnp.bfloat16)

    share = [
        [jnp.where(named[b] == i, jnp.float32(1), jnp.float32(0)) for b in range(BITS)]
        for i in range(BALLS)
    ]

    @pl.loop(0, PAIRS)
    def _(p):
        cols = pl.ds(pl.multiple_of(p * SLAB, SLAB), SLAB)
        for b in range(BITS):
            back(p, b).wait_recv()
        for i in range(BALLS):
            ak, av = gk[p, i], gv[p, i]
            for b in range(BITS):
                ak = ak + share[i][b] * brecv[p, 0, b].astype(jnp.float32)
                av = av + share[i][b] * brecv[p, 1, b].astype(jnp.float32)
            out[1, i, :, cols] = ak.astype(jnp.bfloat16)
            out[2, i, :, cols] = av.astype(jnp.bfloat16)

    @pl.loop(0, PAIRS)
    def _(p):
        for b in range(BITS):
            ahead(p, b).wait_send()
            back(p, b).wait_send()


def deliver(grads, oq_ref, ok_ref, ov_ref, sem):
    copies = [
        pltpu.make_async_copy(grads.at[n, i], dst.at[i], sem.at[n, i])
        for n, dst in enumerate((oq_ref, ok_ref, ov_ref))
        for i in range(BALLS)
    ]
    for copy in copies:
        copy.start()
    for copy in copies:
        copy.wait()


def body(query_rows, key_rows, value_rows, grad_out, partner_balls):
    vmem = pl.BlockSpec(memory_space=pltpu.VMEM)
    hbm = pl.BlockSpec(memory_space=pltpu.HBM)
    balls = jax.ShapeDtypeStruct((BALLS, BALL, WIDTH), jnp.bfloat16)
    link = pltpu.VMEM((PAIRS, 2, BITS, BALL, SLAB), jnp.bfloat16)
    sem = pltpu.SemaphoreType.DMA((PAIRS, BITS))
    near = pltpu.VMEM((PAIRS, BALLS, BALL, SLAB), jnp.float32)
    rows = pltpu.VMEM((BALLS, BALL, WIDTH), jnp.bfloat16)
    grads = pl.pallas_call(
        kernel,
        out_shape=pltpu.VMEM((3, BALLS, BALL, WIDTH), jnp.bfloat16),
        in_specs=[hbm] * 5,
        out_specs=vmem,
        scratch_shapes=[
            pltpu.SMEM((BALLS, BALLS * 32), jnp.int32),
            rows, rows, rows, rows,
            link, link, link, link,
            pltpu.VMEM((BITS, 8, ROWS), jnp.float32),
            pltpu.VMEM((2 * ROWS, SLAB), jnp.bfloat16),
            pltpu.VMEM((2 * ROWS, SLAB), jnp.bfloat16),
            pltpu.VMEM((SLAB, KEYS), jnp.bfloat16),
            pltpu.VMEM((BALLS + BITS, BALL, QB), jnp.float32),
            pltpu.VMEM((BALLS + BITS, BALL, QB), jnp.float32),
            pltpu.VMEM((KEYS, 2 * ROWS), jnp.bfloat16),
            pltpu.VMEM((KEYS, 2 * ROWS), jnp.bfloat16),
            pltpu.VMEM((SLAB, ROWS), jnp.float32),
            near, near,
            sem, sem, sem, sem,
            pltpu.SemaphoreType.DMA,
            pltpu.SemaphoreType.DMA((4, BALLS)),
        ],
        compiler_params=pltpu.CompilerParams(
            collective_id=0, has_side_effects=True, vmem_limit_bytes=40 << 20
        ),
    )(
        pltpu.with_memory_space_constraint(partner_balls.T, pltpu.HBM),
        *(
            pltpu.with_memory_space_constraint(
                x.reshape(BALLS, BALL, WIDTH), pltpu.HBM
            )
            for x in (query_rows, key_rows, value_rows, grad_out)
        ),
    )
    grads = pl.pallas_call(
        deliver,
        out_shape=(balls, balls, balls),
        in_specs=[vmem],
        out_specs=(hbm, hbm, hbm),
        scratch_shapes=[pltpu.SemaphoreType.DMA((3, BALLS))],
        compiler_params=pltpu.CompilerParams(vmem_limit_bytes=8 << 20),
    )(pltpu.with_memory_space_constraint(grads, pltpu.VMEM))
    return tuple(x.reshape(ROWS, WIDTH) for x in grads)


def solution(mesh):
    rows = P(("region", "sub"), None)
    return jax.shard_map(
        body,
        mesh=mesh,
        in_specs=(rows, rows, rows, rows, P("region", None)),
        out_specs=(rows, rows, rows),
        check_vma=False,
    )
```

```python
import functools

import jax
import jax.numpy as jnp
from jax import lax
from jax.experimental import pallas as pl
from jax.experimental.pallas import tpu as pltpu
from jax.sharding import PartitionSpec as P

HEADS = 8
HDIM = 64
BALL = 128
BALLS = 4
BITS = 5
ROWS = BALL * BALLS
WIDTH = HEADS * HDIM
SLAB = 2 * HDIM
PAIRS = HEADS // 2
FAR = BITS * BALL
KEYS = ROWS + FAR
QB = 256
UNITS = 2 * ROWS // QB
MESH = pl.DeviceIdType.MESH
SENDS = (4, 3, 2, 1, 0)
NN = (((1,), (0,)), ((), ()))
NT = (((1,), (1,)), ((), ()))


def mm(a, b, dims):
    return lax.dot_general(a, b, dims, preferred_element_type=jnp.float32)


def kernel(
    pb_hbm, q_hbm, k_hbm, v_hbm, g_hbm, out,
    pb_ref, q_ref, k_ref, v_ref, g_ref, sbuf, rbuf, bsend, brecv, bias, rq, rg, kt, s_scr, dp_scr, p_scr, ds_scr,
    dqt, gk, gv, s_sem, r_sem, bs_sem, br_sem,
    pb_sem, in_sem,
):
    table = pltpu.make_async_copy(pb_hbm, pb_ref, pb_sem)
    table.start()
    fetch = [
        [
            pltpu.make_async_copy(src.at[i], dst.at[i], in_sem.at[n, i])
            for i in range(BALLS)
        ]
        for n, (src, dst) in enumerate(
            ((k_hbm, k_ref), (v_hbm, v_ref), (q_hbm, q_ref), (g_hbm, g_ref))
        )
    ]
    for copies in fetch[:2]:
        for copy in copies:
            copy.start()
    region = lax.axis_index("region")
    me = lax.axis_index("sub")
    deep = me // 4
    peers = [jnp.bitwise_xor(me, 1 << b) for b in range(BITS)]
    barrier = pltpu.get_barrier_semaphore()
    for peer in peers:
        pl.semaphore_signal(
            barrier, inc=1, device_id=(region, peer), device_id_type=MESH
        )

    table.wait()
    named = []
    for b in range(BITS):
        ball = jnp.int32(0)
        for r in range(BALLS):
            for c in range(BALLS):
                entry = pb_ref[c, peers[b] * BALLS + r]
                ball = jnp.where(entry // BALLS == me, entry % BALLS, ball)
        named.append(ball)
    for copies in fetch[:2]:
        for copy in copies:
            copy.wait()
    for copies in fetch[2:]:
        for copy in copies:
            copy.start()
    for b in SENDS:
        kb = k_ref[named[b]]
        vb = v_ref[named[b]]
        for p in range(PAIRS):
            sbuf[p, 0, b] = kb[:, p * SLAB : (p + 1) * SLAB]
            sbuf[p, 1, b] = vb[:, p * SLAB : (p + 1) * SLAB]

    def ahead(p, b):
        return pltpu.make_async_remote_copy(
            src_ref=sbuf.at[p, :, b],
            dst_ref=rbuf.at[p, :, b],
            send_sem=s_sem.at[p, b],
            recv_sem=r_sem.at[p, b],
            device_id=(region, peers[b]),
            device_id_type=MESH,
        )

    def back(p, b):
        return pltpu.make_async_remote_copy(
            src_ref=bsend.at[p, :, b],
            dst_ref=brecv.at[p, :, b],
            send_sem=bs_sem.at[p, b],
            recv_sem=br_sem.at[p, b],
            device_id=(region, peers[b]),
            device_id_type=MESH,
        )

    def give_near(p):
        for b in (3, 2):

            @pl.when(deep // (1 << (b - 2)) % 2 == 1)
            def _():
                back(p, b).start()

        for b in (1, 0):
            back(p, b).start()
        for b in (2, 3):

            @pl.when(deep // (1 << (b - 2)) % 2 == 0)
            def _():
                back(p, b).start()

    def give_late(p):
        @pl.when(deep < 4)
        def _():
            back(p, 4).start()

        @pl.when(deep >= 4)
        def _():
            give_near(p)

    pl.semaphore_wait(barrier, BITS)

    @pl.loop(0, PAIRS)
    def _(p):
        for b in SENDS:
            ahead(p, b).start()

    for b in range(BITS):
        for r in range(BALLS):
            seen = jnp.float32(-1e30)
            for c in range(BALLS):
                entry = pb_ref[c, me * BALLS + r]
                seen = jnp.where(entry // BALLS == peers[b], jnp.float32(0), seen)
            bias[b, :, r * BALL : (r + 1) * BALL] = jnp.full((8, BALL), seen)

    for copies in fetch[2:]:
        for copy in copies:
            copy.wait()
    lane = lax.broadcasted_iota(jnp.int32, (ROWS, SLAB), 1)

    @pl.loop(0, PAIRS)
    def _(p):
        cols = pl.ds(pl.multiple_of(p * SLAB, SLAB), SLAB)
        q = q_ref[:, :, cols].reshape(ROWS, SLAB) * jnp.bfloat16(HDIM**-0.5)
        g = g_ref[:, :, cols].reshape(ROWS, SLAB)
        zero = jnp.zeros_like(q)
        for hh in range(2):
            mine = (lane // HDIM) == hh
            rq[hh * ROWS : (hh + 1) * ROWS] = jnp.where(mine, q, zero)
            rg[hh * ROWS : (hh + 1) * ROWS] = jnp.where(mine, g, zero)
        for i in range(BALLS):
            kt[:, i * BALL : (i + 1) * BALL] = k_ref[i, :, cols].T
        for b in range(BITS):
            ahead(p, b).wait_recv()
        for b in range(BITS):
            kt[:, ROWS + b * BALL : ROWS + (b + 1) * BALL] = rbuf[p, 0, b].T

        def keys_of(i):
            return k_ref[i, :, cols] if i < BALLS else rbuf[p, 0, i - BALLS]

        def values_of(i):
            return v_ref[i, :, cols] if i < BALLS else rbuf[p, 1, i - BALLS]

        @pl.loop(0, UNITS)
        def _(u):
            hh, qb = u // (ROWS // QB), u % (ROWS // QB)
            at = pl.ds(pl.multiple_of(u * QB, QB), QB)
            some = pl.ds(pl.multiple_of(qb * QB, QB), QB)
            head = pl.ds(pl.multiple_of(hh * HDIM, HDIM), HDIM)
            qu = rq[at]
            gu = rg[at]
            top = None
            for i in range(BALLS + BITS):
                s = mm(keys_of(i), qu, NT)
                if i >= BALLS:
                    s = s + bias[i - BALLS, 0:1, some]
                s_scr[i] = s
                m = jnp.max(s.reshape(BALL // 8, 8, QB), axis=0)
                top = m if top is None else jnp.maximum(top, m)
            top = jnp.max(top, axis=0, keepdims=True)
            total = jnp.zeros((8, QB), jnp.float32)
            for i in range(BALLS + BITS):
                dp = mm(values_of(i), gu, NT)
                e = jnp.exp(s_scr[i] - top)
                s_scr[i] = e
                dp_scr[i] = dp
                total = total + jnp.sum(e.reshape(BALL // 8, 8, QB), axis=0)
            scale = 1.0 / jnp.sum(total, axis=0, keepdims=True)
            mean = jnp.zeros((8, QB), jnp.float32)
            for i in range(BALLS + BITS):
                pb = (s_scr[i] * scale).astype(jnp.bfloat16)
                p_scr[i * BALL : (i + 1) * BALL, at] = pb
                part = pb.astype(jnp.float32) * dp_scr[i]
                mean = mean + jnp.sum(part.reshape(BALL // 8, 8, QB), axis=0)
            delta = jnp.sum(mean, axis=0, keepdims=True)
            for i in range(BALLS + BITS):
                ds = s_scr[i] * scale * (dp_scr[i] - delta)
                ds_scr[i * BALL : (i + 1) * BALL, at] = ds.astype(jnp.bfloat16)
            dqt[head, some] = mm(kt[head], ds_scr[:, at], NN)

        for b in range(BITS):
            at = slice(ROWS + b * BALL, ROWS + (b + 1) * BALL)
            bsend[p, 0, b] = mm(ds_scr[at], rq[...], NN).astype(jnp.bfloat16)
            bsend[p, 1, b] = mm(p_scr[at], rg[...], NN).astype(jnp.bfloat16)
        @pl.when(deep < 4)
        def _():
            give_near(p)

        @pl.when(deep >= 4)
        def _():
            back(p, 4).start()

        @pl.when(p > 0)
        def _():
            give_late(p - 1)

        @pl.when(p == PAIRS - 1)
        def _():
            give_late(p)

        for i in range(BALLS):
            at = slice(i * BALL, (i + 1) * BALL)
            gk[p, i] = mm(ds_scr[at], rq[...], NN)
            gv[p, i] = mm(p_scr[at], rg[...], NN)
        for i in range(BALLS):
            dq = dqt[:, i * BALL : (i + 1) * BALL].T * HDIM**-0.5
            out[0, i, :, cols] = dq.astype(jnp.bfloat16)

    share = [
        [jnp.where(named[b] == i, jnp.float32(1), jnp.float32(0)) for b in range(BITS)]
        for i in range(BALLS)
    ]

    @pl.loop(0, PAIRS)
    def _(p):
        cols = pl.ds(pl.multiple_of(p * SLAB, SLAB), SLAB)
        for bits in ((0, 1, 2), (3,)):
            for b in bits:
                back(p, b).wait_recv()
            for i in range(BALLS):
                ak, av = gk[p, i], gv[p, i]
                for b in bits:
                    ak = ak + share[i][b] * brecv[p, 0, b].astype(jnp.float32)
                    av = av + share[i][b] * brecv[p, 1, b].astype(jnp.float32)
                gk[p, i] = ak
                gv[p, i] = av
        back(p, 4).wait_recv()
        for i in range(BALLS):
            ak = gk[p, i] + share[i][4] * brecv[p, 0, 4].astype(jnp.float32)
            av = gv[p, i] + share[i][4] * brecv[p, 1, 4].astype(jnp.float32)
            out[1, i, :, cols] = ak.astype(jnp.bfloat16)
            out[2, i, :, cols] = av.astype(jnp.bfloat16)

    @pl.loop(0, PAIRS)
    def _(p):
        for b in range(BITS):
            ahead(p, b).wait_send()
            back(p, b).wait_send()


def deliver(grads, oq_ref, ok_ref, ov_ref, sem):
    copies = [
        pltpu.make_async_copy(grads.at[n, i], dst.at[i], sem.at[n, i])
        for n, dst in enumerate((oq_ref, ok_ref, ov_ref))
        for i in range(BALLS)
    ]
    for copy in copies:
        copy.start()
    for copy in copies:
        copy.wait()


def body(query_rows, key_rows, value_rows, grad_out, partner_balls):
    vmem = pl.BlockSpec(memory_space=pltpu.VMEM)
    hbm = pl.BlockSpec(memory_space=pltpu.HBM)
    balls = jax.ShapeDtypeStruct((BALLS, BALL, WIDTH), jnp.bfloat16)
    link = pltpu.VMEM((PAIRS, 2, BITS, BALL, SLAB), jnp.bfloat16)
    sem = pltpu.SemaphoreType.DMA((PAIRS, BITS))
    near = pltpu.VMEM((PAIRS, BALLS, BALL, SLAB), jnp.float32)
    rows = pltpu.VMEM((BALLS, BALL, WIDTH), jnp.bfloat16)
    grads = pl.pallas_call(
        kernel,
        out_shape=pltpu.VMEM((3, BALLS, BALL, WIDTH), jnp.bfloat16),
        in_specs=[hbm] * 5,
        out_specs=vmem,
        scratch_shapes=[
            pltpu.SMEM((BALLS, BALLS * 32), jnp.int32),
            rows, rows, rows, rows,
            link, link, link, link,
            pltpu.VMEM((BITS, 8, ROWS), jnp.float32),
            pltpu.VMEM((2 * ROWS, SLAB), jnp.bfloat16),
            pltpu.VMEM((2 * ROWS, SLAB), jnp.bfloat16),
            pltpu.VMEM((SLAB, KEYS), jnp.bfloat16),
            pltpu.VMEM((BALLS + BITS, BALL, QB), jnp.float32),
            pltpu.VMEM((BALLS + BITS, BALL, QB), jnp.float32),
            pltpu.VMEM((KEYS, 2 * ROWS), jnp.bfloat16),
            pltpu.VMEM((KEYS, 2 * ROWS), jnp.bfloat16),
            pltpu.VMEM((SLAB, ROWS), jnp.float32),
            near, near,
            sem, sem, sem, sem,
            pltpu.SemaphoreType.DMA,
            pltpu.SemaphoreType.DMA((4, BALLS)),
        ],
        compiler_params=pltpu.CompilerParams(
            collective_id=0, has_side_effects=True, vmem_limit_bytes=40 << 20
        ),
    )(
        pltpu.with_memory_space_constraint(partner_balls.T, pltpu.HBM),
        *(
            pltpu.with_memory_space_constraint(
                x.reshape(BALLS, BALL, WIDTH), pltpu.HBM
            )
            for x in (query_rows, key_rows, value_rows, grad_out)
        ),
    )
    grads = pl.pallas_call(
        deliver,
        out_shape=(balls, balls, balls),
        in_specs=[vmem],
        out_specs=(hbm, hbm, hbm),
        scratch_shapes=[pltpu.SemaphoreType.DMA((3, BALLS))],
        compiler_params=pltpu.CompilerParams(vmem_limit_bytes=8 << 20),
    )(pltpu.with_memory_space_constraint(grads, pltpu.VMEM))
    return tuple(x.reshape(ROWS, WIDTH) for x in grads)


def solution(mesh):
    rows = P(("region", "sub"), None)
    return jax.shard_map(
        body,
        mesh=mesh,
        in_specs=(rows, rows, rows, rows, P("region", None)),
        out_specs=(rows, rows, rows),
        check_vma=False,
    )
```
